32 devices in a mesh: dp: 8 (over y, x, core), tensor: 4 (over z).
Axes of the slice: x: 2, y: 2, z: 4, core: 2. Of those that a mesh axis runs over, the one named last changes fastest.
Arguments:
- block_input: bfloat16 [4096, 1024], P(('dp', 'tensor')), may hold values from -6 to 6
- segment_ids: int32 [8, 512], P('dp'), may hold values from 0 to 3, never falling along the last dimension, each value on 1 to 256 neighbouring positions
- attention_norm_gain: float32 [1024], replicated, may hold values from 0.1 to 1.9
- w_qkv: bfloat16 [1024, 2048], P('dp', 'tensor'), may hold values from -0.1875 to 0.1875
- w_og: bfloat16 [1024, 1024], P('dp', 'tensor'), may hold values from -0.1875 to 0.1875
- w_beta: bfloat16 [1024, 4], P('dp', 'tensor'), may hold values from -0.1875 to 0.1875
- w_alpha: bfloat16 [1024, 4], P('dp', 'tensor'), may hold values from -0.1875 to 0.1875
- conv_weight: float32 [4, 2048], P(None, 'tensor'), may hold values from -3 to 3
- a_log: float32 [4], P('tensor'), may hold values from -6 to -1
- dt_bias: float32 [4], P('tensor'), may hold values from -2 to 1
- out_gain: float32 [256], replicated, may hold values from 0.1 to 1.9
- w_out: bfloat16 [1024, 1024], P('tensor', 'dp'), may hold values from -0.1875 to 0.1875
- ffn_gain: float32 [1024], replicated, may hold values from 0.1 to 1.9
- w_ffn_gate: bfloat16 [1024, 2816], P('dp', 'tensor'), may hold values from -0.1875 to 0.1875
- w_ffn_up: bfloat16 [1024, 2816], P('dp', 'tensor'), may hold values from -0.1875 to 0.1875
- w_ffn_down: bfloat16 [2816, 1024], P('tensor', 'dp'), may hold values from -0.109375 to 0.109375
- cotangent: bfloat16 [4096, 1024], P(('dp', 'tensor')), may hold values from -6 to 6
Outputs:
- block_output: bfloat16 [4096, 1024], P(('dp', 'tensor'))
- input_grad: float32 [4096, 1024], P(('dp', 'tensor'))
- attn_gain_grad: float32 [1024], replicated
- w_qkv_grad: float32 [1024, 2048], P('dp', 'tensor')
- w_og_grad: float32 [1024, 1024], P('dp', 'tensor')
- w_beta_grad: float32 [1024, 4], P('dp', 'tensor')
- w_alpha_grad: float32 [1024, 4], P('dp', 'tensor')
- conv_weight_grad: float32 [4, 2048], P(None, 'tensor')
- a_log_grad: float32 [4], P('tensor')
- dt_bias_grad: float32 [4], P('tensor')
- out_gain_grad: float32 [256], replicated
- w_out_grad: float32 [1024, 1024], P('tensor', 'dp')
- ffn_gain_grad: float32 [1024], replicated
- w_ffn_gate_grad: float32 [1024, 2816], P('dp', 'tensor')
- w_ffn_up_grad: float32 [1024, 2816], P('dp', 'tensor')
- w_ffn_down_grad: float32 [2816, 1024], P('tensor', 'dp')
The draws below stay inside these ranges and needn't reach their ends.
Inputs may be any that keep to these rules, and one draw needn't show every extreme that they name: `segment_ids`: along each sequence the document ids never fall; each of the 4 documents covers 1 to 256 positions, and some document has exactly 256.
All inputs are finite; a program needn't handle non-finite values.
Results may differ from the reference program's by a relative error of at most 0.012.
Values may be sent and summed in bfloat16 or wider, within the bound.
A program may use at most 128 MiB of HBM per device.

```python
import math
from functools import partial
import jax
import jax.numpy as jnp
import numpy as np
from jax import lax

D = 1024
H = 4
DK = 128
DV = 256
FF = 2816
KC = 4
LEN = 512
DOCS = 4
DOC_MOST = 256
CONV = 2048
HV = 1024
NSEQ = 8
TOKENS = 4096


def steps_of(own_key, shape, pieces, low, high):
    gain = 1.0
    for position, shards_of in pieces:
        heights = jax.random.uniform(jax.random.fold_in(jax.random.fold_in(own_key, 6), position), (shards_of,), jnp.float32, low / len(pieces), high / len(pieces))
        gain = gain * jnp.repeat(jnp.exp(heights), shape[position] // shards_of).reshape((-1,) + (1,) * (len(shape) - 1 - position))
    return gain


def split_up(number_of, total, bound, lean):
    loads = [(1 << 20) // math.isqrt(grade ** lean) + 1 for grade in range(2, number_of + 1)]
    spare, counts = total - bound - (number_of - 1), [1] * (number_of - 1)
    while spare > 0:
        candidates = [i for i in range(number_of - 1) if counts[i] < bound]
        pool, remaining = sum([loads[i] for i in candidates]), spare
        for i in candidates:
            more = min(bound - counts[i], max(1, remaining * loads[i] // pool), spare)
            counts[i] = counts[i] + more
            spare = spare - more
    return np.array([bound] + counts)


def uneven(key, count, total, most, lean):
    if count == 2:
        one = jax.random.randint(key, (), max(1, total - most), min(most, total - 1) + 1)
        return jnp.stack([one, total - one])
    lengths = jnp.asarray(split_up(count, total, most, lean), jnp.int32)
    pairs = (count - 1) // 2
    donor, taker = lengths[1:1 + 2 * pairs:2], lengths[2:2 + 2 * pairs:2]
    margin = jnp.minimum(donor - 1, most - taker)
    moved = jax.random.randint(jax.random.fold_in(key, 1), (pairs,), 0, 1 << 20) % (margin + 1)
    lengths = lengths.at[1:1 + 2 * pairs:2].set(donor - moved).at[2:2 + 2 * pairs:2].set(taker + moved)
    return lengths[jax.random.permutation(jax.random.fold_in(key, 2), count)]


def gaussian(rng, dims, scale, most, shards=(), kind=jnp.bfloat16):
    values = scale * jax.random.normal(rng, dims, jnp.float32)
    if shards:
        values = values * steps_of(rng, dims, shards, -0.22, 0.18)
    return jnp.clip(values, -most, most).astype(kind)


def setup_inputs(seed: int = 0) -> dict:
    key_list = jax.random.split(jax.random.key(seed), 18)
    return {
        "block_input": gaussian(key_list[0], (TOKENS, D), 1.0, 6.0, ((0, 32),)),
        "segment_ids": jax.vmap(lambda own: jnp.searchsorted(jnp.cumsum(uneven(own, DOCS, LEN, DOC_MOST, 0)), jnp.arange(LEN), side="right"))(jax.random.split(key_list[1], NSEQ)).reshape((NSEQ, LEN)).astype(jnp.int32),
        "attention_norm_gain": jnp.clip(1.0 + 0.18 * jax.random.normal(key_list[2], (D,), jnp.float32), 0.1, 1.9),
        "w_qkv": gaussian(key_list[3], (D, CONV), D ** -0.5, 0.1875, ((0, 8), (1, 4))),
        "w_og": gaussian(key_list[4], (D, HV), D ** -0.5, 0.1875, ((0, 8), (1, 4))),
        "w_beta": gaussian(key_list[5], (D, H), D ** -0.5, 0.1875, ((0, 8), (1, 4))),
        "w_alpha": gaussian(key_list[6], (D, H), D ** -0.5, 0.1875, ((0, 8), (1, 4))),
        "conv_weight": gaussian(key_list[7], (KC, CONV), KC ** -0.5, 3.0, ((1, 4),), jnp.float32),
        "a_log": jnp.clip(-6.0 + 5.0 * jax.random.uniform(key_list[8], (H,), jnp.float32) ** steps_of(key_list[8], (H,), ((0, 4),), -0.2, 0.2), -6.0, -1.0),
        "dt_bias": jnp.clip(-2.0 + 3.0 * jax.random.uniform(key_list[9], (H,), jnp.float32) ** steps_of(key_list[9], (H,), ((0, 4),), -0.2, 0.2), -2.0, 1.0),
        "out_gain": jnp.clip(1.0 + 0.18 * jax.random.normal(key_list[10], (DV,), jnp.float32), 0.1, 1.9),
        "w_out": gaussian(key_list[11], (HV, D), HV ** -0.5, 0.1875, ((0, 4), (1, 8))),
        "ffn_gain": jnp.clip(1.0 + 0.18 * jax.random.normal(key_list[12], (D,), jnp.float32), 0.1, 1.9),
        "w_ffn_gate": gaussian(key_list[13], (D, FF), D ** -0.5, 0.1875, ((0, 8), (1, 4))),
        "w_ffn_up": gaussian(key_list[14], (D, FF), D ** -0.5, 0.1875, ((0, 8), (1, 4))),
        "w_ffn_down": gaussian(key_list[15], (FF, D), FF ** -0.5, 0.109375, ((0, 4), (1, 8))),
        "cotangent": gaussian(key_list[16], (TOKENS, D), 1.0, 6.0, ((0, 32),)),
    }


HIGHEST = lax.Precision.HIGHEST

def matmul(left, right):
    return jnp.dot(left, right, preferred_element_type=jnp.float32)

def contract(form, left, right):
    return jnp.einsum(form, left, right, precision=HIGHEST)

def short_conv(mixer_in, conv_weight, segment):
    taps = conv_weight.shape[0]
    total = conv_weight[taps - 1] * mixer_in
    for offset in range(1, taps):
        shifted = jnp.concatenate([jnp.zeros((offset, mixer_in.shape[1]), mixer_in.dtype), mixer_in[:-offset]], 0)
        earlier = jnp.concatenate([jnp.full((offset,), -1, jnp.int32), segment[:-offset]], 0)
        same_doc = (earlier == segment).astype(mixer_in.dtype)
        total = total + conv_weight[taps - 1 - offset] * shifted * same_doc[:, None]
    return jax.nn.silu(total)

def split_heads(activated, heads):
    grouped = activated.reshape(activated.shape[0], heads, 2 * DK + DV)
    query = grouped[..., :DK]
    keys = grouped[..., DK:2 * DK]
    values = grouped[..., 2 * DK:]
    query = query * lax.rsqrt(lax.optimization_barrier(jnp.sum(query * query, -1, keepdims=True)) + 1e-06) * DK ** (-0.5)
    keys = keys * lax.rsqrt(lax.optimization_barrier(jnp.sum(keys * keys, -1, keepdims=True)) + 1e-06)
    return (query, keys, values)

def gated_norm(output_heads, gate_in, out_gain):
    rows, heads = (output_heads.shape[0], output_heads.shape[1])
    gate_heads = gate_in.reshape(rows, heads, DV)
    normed = output_heads * lax.rsqrt(lax.optimization_barrier(jnp.mean(output_heads * output_heads, -1, keepdims=True)) + 1e-05) * out_gain
    return (normed * jax.nn.silu(gate_heads)).reshape(rows, heads * DV)

def mixer_core(segment, mixer_in, gate_in, beta_in, decay_in, conv_weight, a_log, dt_bias, out_gain):
    heads = a_log.shape[0]
    query, keys, values = split_heads(short_conv(mixer_in, conv_weight, segment), heads)
    strength = jax.nn.sigmoid(beta_in)
    log_decay = -jnp.exp(a_log) * jax.nn.softplus(decay_in + dt_bias)
    earlier = jnp.concatenate([jnp.full((1,), -1, jnp.int32), segment[:-1]], 0)
    factor = jnp.exp(log_decay) * (earlier == segment).astype(log_decay.dtype)[:, None]

    def advance(state, inputs):
        query_now, key_now, value_now, strength_now, factor_now = inputs
        decayed = factor_now[:, None, None] * state
        predicted = contract('hvk,hk->hv', decayed, key_now)
        update = strength_now[:, None] * (value_now - predicted)
        state = decayed + update[:, :, None] * key_now[:, None, :]
        return (state, contract('hvk,hk->hv', state, query_now))
    initial = jnp.zeros((heads, DV, DK), mixer_in.dtype)
    _, output_heads = lax.scan(advance, initial, (query, keys, values, strength, factor))
    return gated_norm(output_heads, gate_in, out_gain)

def root_mean_square_forward(rows):
    inverse_scale = lax.rsqrt(lax.optimization_barrier(jnp.mean(rows * rows, -1, keepdims=True)) + 1e-06)
    return (rows * inverse_scale, inverse_scale)

def root_mean_square_backward(normalized_input, inverse_scale, norm_gain, upstream_gradient):
    scaled_rows = upstream_gradient * norm_gain
    return (inverse_scale * (scaled_rows - normalized_input * lax.optimization_barrier(jnp.mean(scaled_rows * normalized_input, -1, keepdims=True))), lax.optimization_barrier(jnp.sum(upstream_gradient * normalized_input, 0)))

def reference(block_input, segment_ids, attention_norm_gain, w_qkv, w_og, w_beta, w_alpha, conv_weight, a_log, dt_bias, out_gain, w_out, ffn_gain, w_ffn_gate, w_ffn_up, w_ffn_down, cotangent):
    shapes = [attention_norm_gain, w_qkv, w_og, w_beta, w_alpha, conv_weight, a_log, dt_bias, out_gain, w_out, ffn_gain, w_ffn_gate, w_ffn_up, w_ffn_down]
    zero_grads = tuple((jnp.zeros(item.shape, jnp.float32) for item in shapes))

    def one_sequence(totals, inputs):
        input_seq, segment, grad_seq = inputs
        residual_input = input_seq.astype(jnp.float32)
        attention_normalized_input, attention_scale = root_mean_square_forward(residual_input)
        attention_normed = (attention_normalized_input * attention_norm_gain).astype(jnp.bfloat16)
        mixer_in = matmul(attention_normed, w_qkv)
        gate_in = matmul(attention_normed, w_og)
        beta_in = matmul(attention_normed, w_beta)
        decay_in = matmul(attention_normed, w_alpha)
        mixed_full, core_back = jax.vjp(partial(mixer_core, segment), mixer_in, gate_in, beta_in, decay_in, conv_weight, a_log, dt_bias, out_gain)
        mixed = mixed_full.astype(jnp.bfloat16)
        resid_mid = residual_input + matmul(mixed, w_out)
        hhat, scale_ffn = root_mean_square_forward(resid_mid)
        normed_ffn = (hhat * ffn_gain).astype(jnp.bfloat16)
        fgate = matmul(normed_ffn, w_ffn_gate)
        fup = matmul(normed_ffn, w_ffn_up)
        sigma = jax.nn.sigmoid(fgate)
        hidden = (fgate * sigma * fup).astype(jnp.bfloat16)
        out_seq = (resid_mid + matmul(hidden, w_ffn_down)).astype(jnp.bfloat16)
        dhidden = matmul(grad_seq, w_ffn_down.T)
        dfgate = (dhidden * fup * sigma * (1.0 + fgate * (1.0 - sigma))).astype(jnp.bfloat16)
        dfup = (dhidden * fgate * sigma).astype(jnp.bfloat16)
        grad_down = matmul(hidden.T, grad_seq)
        grad_fgate = matmul(normed_ffn.T, dfgate)
        grad_fup = matmul(normed_ffn.T, dfup)
        dnormed_ffn = matmul(dfgate, w_ffn_gate.T) + matmul(dfup, w_ffn_up.T)
        dresid_norm, grad_ffn_gain = root_mean_square_backward(hhat, scale_ffn, ffn_gain, dnormed_ffn)
        dresid = grad_seq.astype(jnp.float32) + dresid_norm
        dresid_b = dresid.astype(jnp.bfloat16)
        grad_out = matmul(mixed.T, dresid_b)
        dmixed = matmul(dresid_b, w_out.T)
        dmixer_f, dgate_f, dbeta_f, ddecay_f, grad_conv, grad_alog, grad_dt, grad_ogain = core_back(dmixed)
        dmixer_b = dmixer_f.astype(jnp.bfloat16)
        dgate_b = dgate_f.astype(jnp.bfloat16)
        dbeta_b = dbeta_f.astype(jnp.bfloat16)
        ddecay_b = ddecay_f.astype(jnp.bfloat16)
        grad_qkv = matmul(attention_normed.T, dmixer_b)
        grad_og = matmul(attention_normed.T, dgate_b)
        grad_beta = matmul(attention_normed.T, dbeta_b)
        grad_alpha = matmul(attention_normed.T, ddecay_b)
        attention_normed_gradient = matmul(dmixer_b, w_qkv.T) + matmul(dgate_b, w_og.T) + matmul(dbeta_b, w_beta.T) + matmul(ddecay_b, w_alpha.T)
        norm_input_gradient, attention_gain_gradient = root_mean_square_backward(attention_normalized_input, attention_scale, attention_norm_gain, attention_normed_gradient)
        input_grad_seq = dresid + norm_input_gradient
        new_grads = (attention_gain_gradient, grad_qkv, grad_og, grad_beta, grad_alpha, grad_conv, grad_alog, grad_dt, grad_ogain, grad_out, grad_ffn_gain, grad_fgate, grad_fup, grad_down)
        totals = jax.tree.map(lambda left, right: left + right.astype(left.dtype), totals, new_grads)
        return (totals, (out_seq, input_grad_seq))
    input_seqs = block_input.reshape(NSEQ, LEN, D)
    grad_seqs = cotangent.reshape(NSEQ, LEN, D)
    totals, (out_all, input_grad_all) = lax.scan(one_sequence, zero_grads, (input_seqs, segment_ids, grad_seqs))
    return (out_all.reshape(TOKENS, D), input_grad_all.reshape(TOKENS, D), totals[0], totals[1], totals[2], totals[3], totals[4], totals[5], totals[6], totals[7], totals[8], totals[9], totals[10], totals[11], totals[12], totals[13])
```

```python
import jax
import jax.numpy as jnp
from jax import lax
from jax.experimental import pallas as pl
from jax.sharding import PartitionSpec as P

DK = 128
DV = 256
STRETCH = 128
LEN = 512


HIGHEST = lax.Precision.HIGHEST


def matmul(left, right):
    return jnp.dot(left, right, preferred_element_type=jnp.float32)


def short_conv(mixer_in, conv_weight, segment):
    taps = conv_weight.shape[0]
    total = conv_weight[taps - 1] * mixer_in
    for offset in range(1, taps):
        shifted = jnp.concatenate(
            [jnp.zeros((offset, mixer_in.shape[1]), mixer_in.dtype), mixer_in[:-offset]], 0
        )
        earlier = jnp.concatenate([jnp.full((offset,), -1, jnp.int32), segment[:-offset]], 0)
        same_doc = (earlier == segment).astype(mixer_in.dtype)
        total = total + conv_weight[taps - 1 - offset] * shifted * same_doc[:, None]
    return jax.nn.silu(total)


def split_heads(activated, heads):
    grouped = activated.reshape(activated.shape[0], heads, 2 * DK + DV)
    query = grouped[..., :DK]
    keys = grouped[..., DK : 2 * DK]
    values = grouped[..., 2 * DK :]
    query = query * lax.rsqrt(jnp.sum(query * query, -1, keepdims=True) + 1e-06) * DK ** (-0.5)
    keys = keys * lax.rsqrt(jnp.sum(keys * keys, -1, keepdims=True) + 1e-06)
    return (query, keys, values)


def gated_norm(output_heads, gate_in, out_gain):
    rows, heads = (output_heads.shape[0], output_heads.shape[1])
    gate_heads = gate_in.reshape(rows, heads, DV)
    normed = (
        output_heads
        * lax.rsqrt(jnp.mean(output_heads * output_heads, -1, keepdims=True) + 1e-05)
        * out_gain
    )
    return (normed * jax.nn.silu(gate_heads)).reshape(rows, heads * DV)


def dot(left, right, left_dim, right_dim):
    return lax.dot_general(
        left,
        right,
        (((left_dim,), (right_dim,)), ((), ())),
        precision=HIGHEST,
        preferred_element_type=jnp.float32,
    )


def strictly_below():
    row = lax.broadcasted_iota(jnp.int32, (STRETCH, STRETCH), 0)
    column = lax.broadcasted_iota(jnp.int32, (STRETCH, STRETCH), 1)
    return row, column


def unit_lower_inverses(lowers):
    row, column = strictly_below()
    span = 1
    results = None
    while span < STRETCH:
        pair = (row // (2 * span) == column // (2 * span)) & (row // span != column // span)
        corners = [jnp.where(pair, lower, 0.0) for lower in lowers]
        if results is None:
            identity = (row == column).astype(jnp.float32)
            results = [identity - corner for corner in corners]
        else:
            halves = [dot(corner, result, 1, 0) for corner, result in zip(corners, results)]
            results = [result - dot(result, half, 1, 0) for result, half in zip(results, halves)]
        span = span * 2
    return results


def forward_kernel(q, k, v, strength, carry, tail, ratio, last, o, u, states, inverses):
    blocks = q.shape[0] // STRETCH
    row, column = strictly_below()
    lowers = []
    for i in range(blocks):
        here = pl.ds(i * STRETCH, STRETCH)
        kk = dot(k[here, :], k[here, :], 1, 1)
        lowers.append(jnp.where(row > column, strength[here, :] * ratio[here, :] * kk, 0.0))
    inverse_list = unit_lower_inverses(lowers)
    state = jnp.zeros((v.shape[1], k.shape[1]), jnp.float32)
    for i in range(blocks):
        here = pl.ds(i * STRETCH, STRETCH)
        states[pl.ds(i * v.shape[1], v.shape[1]), :] = state
        inverses[here, :] = inverse_list[i]
        keys, query, carried = k[here, :], q[here, :], carry[here, :]
        target = strength[here, :] * (v[here, :] - carried * dot(keys, state, 1, 1))
        update = dot(inverse_list[i], target, 1, 0)
        u[here, :] = update
        weights = ratio[here, :] * dot(query, keys, 1, 1)
        o[here, :] = carried * dot(query, state, 1, 1) + dot(weights, update, 1, 0)
        state = last[pl.ds(i, 1), :] * state + dot(update * tail[here, :], keys, 0, 0)


def backward_kernel(
    q, k, v, strength, carry, tail, ratio, last, u, states, inverses, do,
    dq, dk, dv, dstrength, dcarry, dtail, dratio, dlast,
):
    blocks = q.shape[0] // STRETCH
    row, column = strictly_below()
    dstate = jnp.zeros((v.shape[1], k.shape[1]), jnp.float32)
    for i in reversed(range(blocks)):
        here = pl.ds(i * STRETCH, STRETCH)
        state = states[pl.ds(i * v.shape[1], v.shape[1]), :]
        keys, query, carried, beta = k[here, :], q[here, :], carry[here, :], strength[here, :]
        ends, scale, update, grad = tail[here, :], ratio[here, :], u[here, :], do[here, :]
        kk = dot(keys, keys, 1, 1)
        qk = dot(query, keys, 1, 1)
        key_state = dot(keys, state, 1, 1)
        query_state = dot(query, state, 1, 1)
        rest = v[here, :] - carried * key_state
        key_dstate = dot(keys, dstate, 1, 1)
        dupdate = dot(scale * qk, grad, 0, 0) + ends * key_dstate
        dtail[here, :] = jnp.sum(key_dstate * update, -1, keepdims=True)
        dweights = dot(grad, update, 1, 1)
        dqk = dweights * scale
        dtarget = dot(inverses[here, :], dupdate, 0, 0)
        dlower = jnp.where(row > column, -dot(dtarget, update, 1, 1), 0.0)
        dstrength[here, :] = jnp.sum(dtarget * rest, -1, keepdims=True) + jnp.sum(
            dlower * scale * kk, -1, keepdims=True
        )
        drest = beta * dtarget
        dv[here, :] = drest
        dcarry[here, :] = jnp.sum(grad * query_state - drest * key_state, -1, keepdims=True)
        dratio[here, :] = dweights * qk + dlower * beta * kk
        dkk = dlower * beta * scale
        dquery_state = carried * grad
        dkey_state = -carried * drest
        dq[here, :] = dot(dquery_state, state, 1, 0) + dot(dqk, keys, 1, 0)
        dk[here, :] = (
            dot(update * ends, dstate, 1, 0)
            + dot(dqk, query, 0, 0)
            + dot(dkey_state, state, 1, 0)
            + dot(dkk, keys, 1, 0)
            + dot(dkk, keys, 0, 0)
        )
        dlast[pl.ds(i, 1), :] = jnp.sum(dstate * state, 0, keepdims=True)
        dstate = (
            last[pl.ds(i, 1), :] * dstate
            + dot(dquery_state, query, 0, 0)
            + dot(dkey_state, keys, 0, 0)
        )


def shaped(*shapes):
    return tuple(jax.ShapeDtypeStruct(shape, jnp.float32) for shape in shapes)


def run_kernel(kernel, out_shape, arrays):
    rows = arrays[0].shape[0]
    return pl.pallas_call(
        kernel,
        out_shape=out_shape,
        cost_estimate=pl.CostEstimate(
            flops=rows * 80_000_000, transcendentals=0, bytes_accessed=rows * 16384
        ),
    )(*arrays)


def delta_run(arrays):
    q, k, v = arrays[:3]
    rows, wide = v.shape
    blocks = rows // STRETCH
    return run_kernel(
        forward_kernel,
        shaped((rows, wide), (rows, wide), (blocks * wide, k.shape[1]), (rows, STRETCH)),
        arrays,
    )


@jax.custom_vjp
def delta_core(*arrays):
    return delta_run(arrays)[0]


def delta_core_forward(*arrays):
    o, u, states, inverses = delta_run(arrays)
    return o, (arrays, u, states, inverses)


def delta_core_backward(saved, do):
    arrays, u, states, inverses = saved
    return tuple(
        run_kernel(
            backward_kernel,
            shaped(*[array.shape for array in arrays]),
            arrays + (u, states, inverses, do),
        )
    )


delta_core.defvjp(delta_core_forward, delta_core_backward)


def delta_blocks(query, keys, values, strength, log_decay, segment):
    rows, heads = (query.shape[0], query.shape[1])
    blocks = rows // STRETCH
    seg = segment.reshape(blocks, STRETCH)
    before = jnp.concatenate([jnp.full((1,), -1, jnp.int32), seg[:-1, -1]], 0)
    position = jnp.arange(STRETCH)
    inclusive = position[:, None] >= position[None, :]
    keep = (seg[:, :, None] == seg[:, None, :]) & inclusive
    at_start = (seg == before[:, None]).astype(jnp.float32)
    outs = []
    for head in range(heads):
        decay = log_decay[:, head].reshape(blocks, STRETCH)
        cumulative = jnp.sum(jnp.where(inclusive, decay[:, None, :], 0.0), -1)
        ratio = jnp.exp(
            jnp.where(keep, cumulative[:, :, None] - cumulative[:, None, :], 0.0)
        ) * keep.astype(jnp.float32)
        carry = jnp.exp(cumulative) * at_start
        outs.append(
            delta_core(
                query[:, head],
                keys[:, head],
                values[:, head],
                strength[:, head][:, None],
                carry.reshape(rows, 1),
                ratio[:, -1, :].reshape(rows, 1),
                ratio.reshape(rows, STRETCH),
                jnp.broadcast_to(carry[:, -1:], (blocks, query.shape[-1])),
            )
        )
    return jnp.stack(outs, 1)


def mixer_core(
    segment, mixer_in, gate_in, beta_in, decay_in, conv_weight, a_log, dt_bias, out_gain
):
    heads = a_log.shape[0]
    query, keys, values = split_heads(short_conv(mixer_in, conv_weight, segment), heads)
    strength = jax.nn.sigmoid(beta_in)
    log_decay = -jnp.exp(a_log) * jax.nn.softplus(decay_in + dt_bias)
    output_heads = delta_blocks(query, keys, values, strength, log_decay, segment)
    return gated_norm(output_heads, gate_in, out_gain)


def root_mean_square_forward(rows):
    inverse_scale = lax.rsqrt(jnp.mean(rows * rows, -1, keepdims=True) + 1e-06)
    return (rows * inverse_scale, inverse_scale)


def root_mean_square_backward(normalized_input, inverse_scale, norm_gain, upstream_gradient):
    scaled_rows = upstream_gradient * norm_gain
    return (
        inverse_scale
        * (
            scaled_rows
            - normalized_input * jnp.mean(scaled_rows * normalized_input, -1, keepdims=True)
        ),
        jnp.sum(upstream_gradient * normalized_input, 0),
    )


def matmul_t(left, right):
    return lax.dot_general(
        left, right, (((1,), (1,)), ((), ())), preferred_element_type=jnp.float32
    )


def scatter_sum(partial_sums, axis):
    count = lax.axis_size(axis)
    rows, columns = partial_sums.shape
    pieces = partial_sums.astype(jnp.bfloat16).reshape(count, rows // count, columns)
    received = lax.all_to_all(pieces, axis, 0, 0)
    return jnp.sum(received.astype(jnp.float32), 0)


def local(
    block_input,
    segment_ids,
    attention_norm_gain,
    w_qkv,
    w_og,
    w_beta,
    w_alpha,
    conv_weight,
    a_log,
    dt_bias,
    out_gain,
    w_out,
    ffn_gain,
    w_ffn_gate,
    w_ffn_up,
    w_ffn_down,
    cotangent,
):
    tensor_count = lax.axis_size("tensor")
    local_rows = block_input.shape[0]
    wide_qkv, wide_og, heads_here = w_qkv.shape[1], w_og.shape[1], w_beta.shape[1]
    wide_in = wide_qkv + wide_og + 2 * heads_here
    hidden_here = w_ffn_gate.shape[1]
    residual_input = block_input.astype(jnp.float32)
    attention_normalized_input, attention_scale = root_mean_square_forward(residual_input)
    local_normed_rows = (attention_normalized_input * attention_norm_gain).astype(jnp.bfloat16)
    attention_normed = lax.all_gather(local_normed_rows, "tensor", axis=0, tiled=True)
    full_mixer = lax.all_gather(
        jnp.concatenate([w_qkv, w_og, w_beta, w_alpha, w_out.T], 1), "dp", axis=0, tiled=True
    )
    full_in, full_out_t = full_mixer[:, :wide_in], full_mixer[:, wide_in:]
    full_ffn = lax.all_gather(
        jnp.concatenate([w_ffn_gate, w_ffn_up, w_ffn_down.T], 1), "dp", axis=0, tiled=True
    )
    full_gate_up, full_down_t = full_ffn[:, : 2 * hidden_here], full_ffn[:, 2 * hidden_here :]
    grad_all = lax.all_gather(cotangent, "tensor", axis=0, tiled=True)
    rows_all = attention_normed.shape[0]
    seq_count = rows_all // LEN
    projected = matmul(attention_normed, full_in).reshape(seq_count, LEN, -1)
    cuts = (wide_qkv, wide_qkv + wide_og, wide_qkv + wide_og + heads_here)

    def core_all(projected, conv_weight, a_log, dt_bias, out_gain):
        mixer_in, gate_in, beta_in, decay_in = jnp.split(projected, cuts, axis=-1)
        return jnp.stack(
            [
                mixer_core(
                    segment_ids[i], mixer_in[i], gate_in[i], beta_in[i], decay_in[i],
                    conv_weight, a_log, dt_bias, out_gain,
                )
                for i in range(seq_count)
            ]
        )

    mixed_full, core_back = jax.vjp(core_all, projected, conv_weight, a_log, dt_bias, out_gain)
    mixed = mixed_full.reshape(rows_all, -1).astype(jnp.bfloat16)
    resid_mid = residual_input + scatter_sum(matmul_t(mixed, full_out_t), "tensor")
    hhat, scale_ffn = root_mean_square_forward(resid_mid)
    normed_ffn_local = (hhat * ffn_gain).astype(jnp.bfloat16)
    normed_ffn = lax.all_gather(normed_ffn_local, "tensor", axis=0, tiled=True)
    gate_up = matmul(normed_ffn, full_gate_up)
    fgate, fup = gate_up[:, :hidden_here], gate_up[:, hidden_here:]
    dhidden = matmul(grad_all, full_down_t)
    sigma = jax.nn.sigmoid(fgate)
    hidden = (fgate * sigma * fup).astype(jnp.bfloat16)
    dfgate = (dhidden * fup * sigma * (1.0 + fgate * (1.0 - sigma))).astype(jnp.bfloat16)
    dfup = (dhidden * fgate * sigma).astype(jnp.bfloat16)
    dgate_up = jnp.concatenate([dfgate, dfup], 1)
    dnormed_ffn = scatter_sum(matmul_t(dgate_up, full_gate_up), "tensor")
    block_output = (
        resid_mid + scatter_sum(matmul_t(hidden, full_down_t), "tensor")
    ).astype(jnp.bfloat16)
    ffn_summed = scatter_sum(
        jnp.concatenate(
            [matmul(normed_ffn.T, dfgate), matmul(normed_ffn.T, dfup), matmul(grad_all.T, hidden)], 1
        ),
        "dp",
    )
    dresid_norm, grad_ffn_gain = root_mean_square_backward(hhat, scale_ffn, ffn_gain, dnormed_ffn)
    dresid = cotangent.astype(jnp.float32) + dresid_norm
    dresid_b = dresid.astype(jnp.bfloat16)
    dresid_all = lax.all_gather(dresid_b, "tensor", axis=0, tiled=True)
    dmixed = matmul(dresid_all, full_out_t).reshape(seq_count, LEN, -1)
    dprojected, grad_conv, grad_alog, grad_dt, grad_ogain = core_back(dmixed)
    dprojected_b = dprojected.reshape(rows_all, -1).astype(jnp.bfloat16)
    attention_normed_gradient = scatter_sum(matmul_t(dprojected_b, full_in), "tensor")
    mixer_summed = scatter_sum(
        jnp.concatenate(
            [matmul(attention_normed.T, dprojected_b), matmul(dresid_all.T, mixed)], 1
        ),
        "dp",
    )
    norm_input_gradient, attention_gain_gradient = root_mean_square_backward(
        attention_normalized_input, attention_scale, attention_norm_gain, attention_normed_gradient
    )
    input_grad = dresid + norm_input_gradient
    everywhere = [attention_gain_gradient, grad_ffn_gain, grad_ogain]
    here = [grad_conv.reshape(-1), grad_alog, grad_dt]
    lengths = [item.shape[0] for item in everywhere + here]
    ends = [sum(lengths[: i + 1]) for i in range(len(lengths))]
    packed = jnp.concatenate(everywhere + here)
    packed = jnp.pad(packed, (0, -packed.shape[0] % 1024)).reshape(8, -1)
    gathered = lax.all_gather(packed, ("dp", "tensor"), axis=0, tiled=True)
    gathered = gathered.reshape(-1, tensor_count, packed.size)
    by_place = jnp.sum(gathered, 0)
    attn_gain_grad, ffn_gain_grad, out_gain_grad = jnp.split(
        jnp.sum(by_place[:, : ends[2]], 0), ends[:2]
    )
    own = lax.dynamic_index_in_dim(by_place, lax.axis_index("tensor"), 0, keepdims=False)
    conv_weight_grad = own[ends[2] : ends[3]].reshape(conv_weight.shape)
    a_log_grad = own[ends[3] : ends[4]]
    dt_bias_grad = own[ends[4] : ends[5]]
    return (
        block_output,
        input_grad,
        attn_gain_grad,
        mixer_summed[:, : cuts[0]],
        mixer_summed[:, cuts[0] : cuts[1]],
        mixer_summed[:, cuts[1] : cuts[2]],
        mixer_summed[:, cuts[2] : wide_in],
        conv_weight_grad,
        a_log_grad,
        dt_bias_grad,
        out_gain_grad,
        mixer_summed[:, wide_in:].T,
        ffn_gain_grad,
        ffn_summed[:, :hidden_here],
        ffn_summed[:, hidden_here : 2 * hidden_here],
        ffn_summed[:, 2 * hidden_here :].T,
    )


def solution(mesh):
    placed = (
        P(("dp", "tensor"), None),
        P("dp", None),
        P(),
        P("dp", "tensor"),
        P("dp", "tensor"),
        P("dp", "tensor"),
        P("dp", "tensor"),
        P(None, "tensor"),
        P("tensor"),
        P("tensor"),
        P(),
        P("tensor", "dp"),
        P(),
        P("dp", "tensor"),
        P("dp", "tensor"),
        P("tensor", "dp"),
        P(("dp", "tensor"), None),
    )
    return jax.shard_map(
        local,
        mesh=mesh,
        in_specs=placed,
        out_specs=(
            P(("dp", "tensor"), None),
            P(("dp", "tensor"), None),
            P(),
            P("dp", "tensor"),
            P("dp", "tensor"),
            P("dp", "tensor"),
            P("dp", "tensor"),
            P(None, "tensor"),
            P("tensor"),
            P("tensor"),
            P(),
            P("tensor", "dp"),
            P(),
            P("dp", "tensor"),
            P("dp", "tensor"),
            P("tensor", "dp"),
        ),
        check_vma=False,
    )
```
